32 devices in a mesh: grid: 8 (over z, y), bead: 4 (over x, core).
Axes of the slice: x: 2, y: 2, z: 4, core: 2. Of those that a mesh axis runs over, the one named last changes fastest.
Arguments:
- positions: float32 [3, 32, 4096], P(None, 'bead', 'grid'), may hold values from -6 to 6
- momenta: float32 [3, 32, 4096], P(None, 'bead', 'grid'), may hold values from -6 to 6
- noise: float32 [3, 32, 4096], P(None, 'bead', 'grid'), may hold values from -6 to 6
- charges: float32 [4096], P('grid'), may hold values from -5 to 5
- slab_route: int32 [4096, 1], P('grid'), may hold values from 0 to 7; in each aligned block of 512 rows (0 to 511, 512 to 1023, ...) at most 128 rows name the same one
- cells: int32 [3, 4096], P(None, 'grid'), may hold values from 0 to 255, as said below
- offsets: float32 [3, 4096], P(None, 'grid'), may hold values from 0 to 0.999
- nbr_tiles: int32 [32, 4], P('grid'), may hold values from 0 to 3
Outputs:
- new_positions: float32 [3, 32, 4096], P(None, 'bead', 'grid')
- new_momenta: float32 [3, 32, 4096], P(None, 'bead', 'grid')
The draws below stay inside these ranges and needn't reach their ends.
Inputs may be any that keep to these rules, and one draw needn't show every extreme that they name: `slab_route`: among the 512 atoms of one domain at most 128 name the same slab, a bound that some block reaches of them. `cells`: row 0 lies below 32, row 1 below 256, row 2 below 256. `nbr_tiles`: tile numbers within the domain of the listing tile.
All inputs are finite; a program needn't handle non-finite values.
Results may differ from the reference program's by a relative error of at most 0.0003.
Values sent between devices are 32-bit elements; how exact they have to be, the bound alone decides.
A program may use at most 64 MiB of HBM per device.

```python
import math
import jax
import jax.numpy as jnp
import numpy as np
from jax import lax

GX = 256
GY = 256
GZ = 256
BEADS = 32
TILE = 128
NBR = 4
ATOM_DEV = 512
SLABS = 8
PLANES = 32
TILE_DEV = 4
CAP = 128
ATOMS = 4096


def draw_cells(key, part):
    keys = jax.random.split(jax.random.fold_in(key, 17), 3)
    plane_draw = jax.random.randint(keys[0], (ATOMS,), 0, PLANES)
    second_draw = jax.random.randint(keys[1], (ATOMS,), 0, GY)
    third_draw = jax.random.randint(keys[2], (ATOMS,), 0, GZ)
    return jnp.stack([plane_draw, second_draw, third_draw]).astype(jnp.int32)


def plant(values, key, least, high):
    longest = values.shape.index(max(values.shape))
    spots = []
    for shift in (0, 1):
        where = [jax.random.randint(jax.random.fold_in(key, axis), (), 0, length) for axis, length in enumerate(values.shape)]
        where[longest] = (where[longest] + shift) % values.shape[longest]
        spots.append(tuple(where))
    return values.at[spots[0]].set(least).at[spots[1]].set(high)


def levels(key, shape, cuts, least, high):
    gain, own = 1.0, jax.random.fold_in(key, 6)
    for axis_at, parts in cuts:
        steps = jnp.exp(jax.random.uniform(jax.random.fold_in(own, axis_at), (parts,), jnp.float32, least / len(cuts), high / len(cuts)))
        gain = gain * jnp.repeat(steps, shape[axis_at] // parts).reshape([-1 if axis == axis_at else 1 for axis in range(len(shape))])
    return gain


def shared_out(key, own, number, rows, count, top, reach, skew):
    order = jax.random.permutation(key, count)
    packed, common = load_shares(count, rows * top, reach, skew, True), load_shares(count, rows * top, reach, skew, False)
    places = jnp.arange(count)

    def named(lengths, turn):
        used = int((lengths > 0).sum())
        fixed = max(1, used // 4)
        moved = fixed + (places - fixed + turn * (used - fixed)) % max(1, count - fixed)
        return jnp.zeros((count,), jnp.int32).at[order[jnp.where(places < fixed, places, moved)]].set(jnp.asarray(lengths, jnp.int32))

    lengths = jnp.where(number % 4 == 0, named(packed, number // 4), named(common, number - number // 4 - 1))
    mixed = jax.random.permutation(jax.random.fold_in(own, 3), count)
    source_of, sink = mixed[0:count // 2 * 2:2], mixed[1:count // 2 * 2:2]
    slack = jnp.minimum(lengths[source_of] - 1, reach - lengths[sink]) // 2
    slack = jnp.where((source_of == order[0]) | (sink == order[0]) | (lengths[sink] == 0), 0, jnp.maximum(slack, 0))
    moved = jax.random.randint(jax.random.fold_in(own, 4), (count // 2,), 0, 1 << 20) % (slack + 1)
    lengths = lengths.at[source_of].add(-moved).at[sink].add(moved)
    members = jnp.searchsorted(jnp.cumsum(lengths), jnp.arange(rows * top), side="right").astype(jnp.int32)
    table = members.reshape(top, rows).T
    table = table[jax.random.permutation(jax.random.fold_in(own, 1), rows)]
    turn = jax.random.randint(jax.random.fold_in(own, 2), (rows, 1), 0, top)
    return jnp.take_along_axis(table, (jnp.arange(top)[None, :] + turn) % top, axis=1)


def load_shares(count, total, reach, skew, full):
    loads = [(1 << 20) // math.isqrt(rank ** skew) + 1 for rank in range(1, count + 1)]
    largest = reach if full else min(reach, max(-(-total // count), total * loads[0] // sum(loads)))
    least = 1 if total - largest >= count - 1 else 0
    given, surplus = [largest] + [least] * (count - 1), total - largest - least * (count - 1)
    while surplus > 0:
        candidates = [i for i in range(1, count) if given[i] < largest] or [i for i in range(1, count) if given[i] < reach]
        whole, budget = sum([loads[i] for i in candidates]), surplus
        for i in candidates:
            more = min(reach - given[i], max(1, budget * loads[i] // whole), surplus)
            given[i] = given[i] + more
            surplus = surplus - more
    return np.array(given)


def normal_values(rng, dims, deviation, bound, cuts=(), kind=jnp.bfloat16):
    drawn = jax.random.normal(rng, dims, jnp.float32) * deviation
    if len(cuts) > 0:
        drawn = levels(rng, dims, cuts, -0.22, 0.18) * drawn
    return jnp.clip(drawn, min=-bound, max=bound).astype(kind)


def setup_inputs(seed: int = 0) -> dict:
    streams_of = jax.random.split(jax.random.key(seed), 9)
    positions = normal_values(streams_of[0], (3, BEADS, ATOMS), 1.0, 6.0, ((1, 4), (2, 8)), jnp.float32)
    momenta = normal_values(streams_of[1], (3, BEADS, ATOMS), 1.0, 6.0, ((1, 4), (2, 8)), jnp.float32)
    noise = normal_values(streams_of[2], (3, BEADS, ATOMS), 1.0, 6.0, ((1, 4), (2, 8)), jnp.float32)
    charges = normal_values(streams_of[3], (ATOMS,), 1.0, 5.0, ((0, 8),), jnp.float32)
    slab_route_keys = jax.random.split(jax.random.fold_in(streams_of[4], 1), ATOMS // ATOM_DEV)
    slab_route_turns = jax.random.permutation(jax.random.fold_in(streams_of[4], 3), ATOMS // ATOM_DEV)
    slab_route = jax.vmap(lambda own, number: shared_out(jax.random.fold_in(streams_of[4], 2), own, number, ATOM_DEV, SLABS, 1, CAP, 2))(slab_route_keys, slab_route_turns).reshape((ATOMS, 1))
    cells = draw_cells(jax.random.fold_in(streams_of[8], 71), 0)
    offsets = jnp.clip(0.999 * jax.random.uniform(streams_of[6], (3, ATOMS), jnp.float32) ** levels(streams_of[6], (3, ATOMS), ((1, 8),), -0.2, 0.2), 0.0, 0.999)
    nbr_tiles = plant(jax.random.randint(streams_of[7], (SLABS * TILE_DEV, NBR), 0, TILE_DEV), jax.random.fold_in(streams_of[7], 1), 0, TILE_DEV - 1).astype(jnp.int32)
    return {"positions": positions, "momenta": momenta, "noise": noise, "charges": charges, "slab_route": slab_route, "cells": cells, "offsets": offsets, "nbr_tiles": nbr_tiles}


highest = lax.Precision.HIGHEST
time_step = 0.5
polymer_frequency = 1.0
centroid_friction = 0.5
coulomb_scale = 100000.0
screen_width = 200.0
pair_strength = 1.0 / 128.0
pair_range = 4.0

def spline(fraction):
    remain = 1.0 - fraction
    square = fraction * fraction
    cubic = square * fraction
    values = [remain * remain * remain / 6.0, (3.0 * cubic - 6.0 * square + 4.0) / 6.0, (-3.0 * cubic + 3.0 * square + 3.0 * fraction + 1.0) / 6.0, cubic / 6.0]
    slopes = [-0.5 * remain * remain, 0.5 * (3.0 * square - 4.0 * fraction), 0.5 * (-3.0 * square + 2.0 * fraction + 1.0), 0.5 * square]
    return (values, slopes)

def influence(index_x, index_y, index_z):
    wave_x = ((index_x + GX // 2) % GX - GX // 2).astype(jnp.float32)
    wave_y = ((index_y + GY // 2) % GY - GY // 2).astype(jnp.float32)
    wave_z = ((index_z + GZ // 2) % GZ - GZ // 2).astype(jnp.float32)
    wave_square = wave_x * wave_x + wave_y * wave_y + wave_z * wave_z
    centre = wave_square == 0.0
    safe_square = jnp.where(centre, 1.0, wave_square)
    return jnp.where(centre, 0.0, coulomb_scale * jnp.exp(-wave_square / (2.0 * screen_width * screen_width)) / safe_square)

def pair_force(centre, beside_all):
    separation = centre[:, :, :, None] - beside_all[:, :, None, :]
    distance_sq = lax.optimization_barrier(jnp.sum(separation * separation, axis=0))
    weight = pair_strength * jnp.exp(-distance_sq / pair_range)
    return lax.optimization_barrier(jnp.sum(weight[None] * separation, axis=3))

def domain_force(local_positions, neighbours):
    tile_count = neighbours.shape[0]
    bead_total = local_positions.shape[1]
    shaped = local_positions.reshape(3, bead_total, tile_count, TILE)

    def one_tile(tile_index):
        centre = lax.dynamic_index_in_dim(shaped, tile_index, 2, keepdims=False)
        beside_all = jnp.take(shaped, neighbours[tile_index], axis=2).reshape(3, bead_total, NBR * TILE)
        return pair_force(centre, beside_all)
    forces = lax.map(one_tile, jnp.arange(tile_count, dtype=jnp.int32))
    return jnp.moveaxis(forces, 0, 2).reshape(3, bead_total, tile_count * TILE)

def mode_matrix(bead_total):
    mode_index = jnp.arange(bead_total, dtype=jnp.int32)[:, None]
    bead_index = jnp.arange(bead_total, dtype=jnp.int32)[None, :]
    angle = (mode_index * bead_index % bead_total).astype(jnp.float32) * (2.0 * math.pi / bead_total)
    middle = bead_total // 2
    first = jnp.full(angle.shape, 1.0 / math.sqrt(bead_total), jnp.float32)
    scaled = math.sqrt(2.0 / bead_total)
    return jnp.where(mode_index == 0, first, jnp.where(mode_index < middle, scaled * jnp.cos(angle), jnp.where(mode_index == middle, jnp.cos(angle) / math.sqrt(bead_total), scaled * jnp.sin(angle))))

def evolve(position_modes, momentum_modes, kicks, mode_index, bead_total):
    frequency = (2.0 * polymer_frequency * jnp.sin(mode_index.astype(jnp.float32) * (math.pi / bead_total)))[None, :, None]
    centroid = (mode_index == 0)[None, :, None]
    half_step = 0.5 * time_step
    cosine_term = jnp.cos(frequency * half_step)
    sine_term = jnp.sin(frequency * half_step)
    safe_frequency = jnp.where(centroid, 1.0, frequency)
    drift_factor = jnp.where(centroid, half_step, sine_term / safe_frequency)

    def rotate(moved_q, moved_p):
        return (moved_q * cosine_term + moved_p * drift_factor, moved_p * cosine_term - moved_q * frequency * sine_term)
    position_modes, momentum_modes = rotate(position_modes, momentum_modes)
    friction = jnp.where(centroid, centroid_friction, 2.0 * frequency)
    damping = jnp.exp(-friction * time_step)
    momentum_modes = damping * momentum_modes + jnp.sqrt(1.0 - damping * damping) * kicks
    return rotate(position_modes, momentum_modes)

def grid_positions(target, cells, offsets, planes):
    first = (target * planes + cells[0]).astype(jnp.float32) + offsets[0]
    second = cells[1].astype(jnp.float32) + offsets[1]
    third = cells[2].astype(jnp.float32) + offsets[2]
    return jnp.stack([first, second, third])

def reference(positions, momenta, noise, charges, slab_route, cells, offsets, nbr_tiles):

    def domain_term(domain):
        domain_block = lax.dynamic_slice_in_dim(positions, domain * ATOM_DEV, ATOM_DEV, 2)
        domain_lists = lax.dynamic_slice_in_dim(nbr_tiles, domain * TILE_DEV, TILE_DEV, 0)
        return domain_force(domain_block, domain_lists)
    short_force = lax.map(domain_term, jnp.arange(SLABS, dtype=jnp.int32))
    short_force = jnp.moveaxis(short_force, 0, 2).reshape(3, BEADS, ATOMS)
    grid_pos = grid_positions(slab_route[:, 0], cells, offsets, PLANES)
    lowest = jnp.floor(grid_pos)
    fraction = grid_pos - lowest
    lowest_int = lowest.astype(jnp.int32)
    values, slopes = spline(fraction)
    charge_grid = jnp.zeros((GX, GY, GZ), jnp.float32)
    for step_x in range(4):
        cell_x = (lowest_int[0] + step_x - 1) % GX
        for step_y in range(4):
            cell_y = (lowest_int[1] + step_y - 1) % GY
            for step_z in range(4):
                cell_z = (lowest_int[2] + step_z - 1) % GZ
                amount = charges * values[step_x][0] * values[step_y][1] * values[step_z][2]
                charge_grid = charge_grid.at[cell_x, cell_y, cell_z].add(amount)
    screen = influence(jnp.arange(GX, dtype=jnp.int32)[:, None, None], jnp.arange(GY, dtype=jnp.int32)[None, :, None], jnp.arange(GZ, dtype=jnp.int32)[None, None, :])
    spectrum = jnp.fft.fftn(charge_grid)
    potential = jnp.real(jnp.fft.ifftn(spectrum * screen)).astype(jnp.float32)
    force_x = jnp.zeros((ATOMS,), jnp.float32)
    force_y = jnp.zeros((ATOMS,), jnp.float32)
    force_z = jnp.zeros((ATOMS,), jnp.float32)
    for step_x in range(4):
        cell_x = (lowest_int[0] + step_x - 1) % GX
        for step_y in range(4):
            cell_y = (lowest_int[1] + step_y - 1) % GY
            for step_z in range(4):
                cell_z = (lowest_int[2] + step_z - 1) % GZ
                sample = potential[cell_x, cell_y, cell_z]
                force_x = force_x + slopes[step_x][0] * values[step_y][1] * values[step_z][2] * sample
                force_y = force_y + values[step_x][0] * slopes[step_y][1] * values[step_z][2] * sample
                force_z = force_z + values[step_x][0] * values[step_y][1] * slopes[step_z][2] * sample
    mesh_force = -charges[None, :] * jnp.stack([force_x, force_y, force_z])
    kicked = momenta + 0.5 * time_step * (short_force + mesh_force[:, None, :])
    matrix = mode_matrix(BEADS)
    position_modes = jnp.einsum('kb,cba->cka', matrix, positions, precision=highest)
    momentum_modes = jnp.einsum('kb,cba->cka', matrix, kicked, precision=highest)
    position_modes, momentum_modes = evolve(position_modes, momentum_modes, noise, jnp.arange(BEADS, dtype=jnp.int32), BEADS)
    new_positions = jnp.einsum('kb,cka->cba', matrix, position_modes, precision=highest)
    new_momenta = jnp.einsum('kb,cka->cba', matrix, momentum_modes, precision=highest)
    return (new_positions, new_momenta)
```

```python
import functools
import math

import jax
import jax.numpy as jnp
import numpy as np
from jax import lax
from jax.experimental import pallas as pl
from jax.experimental.pallas import tpu as pltpu
from jax.sharding import PartitionSpec as P

GX = 256
GY = 256
GZ = 256
BEADS = 32
TILE = 128
NBR = 4


highest = lax.Precision.HIGHEST
time_step = 0.5
polymer_frequency = 1.0
centroid_friction = 0.5
coulomb_scale = 100000.0
screen_width = 200.0
pair_strength = 1.0 / 128.0
pair_range = 4.0


def spline(fraction):
    remain = 1.0 - fraction
    square = fraction * fraction
    cubic = square * fraction
    values = [
        remain * remain * remain / 6.0,
        (3.0 * cubic - 6.0 * square + 4.0) / 6.0,
        (-3.0 * cubic + 3.0 * square + 3.0 * fraction + 1.0) / 6.0,
        cubic / 6.0,
    ]
    slopes = [
        -0.5 * remain * remain,
        0.5 * (3.0 * square - 4.0 * fraction),
        0.5 * (-3.0 * square + 2.0 * fraction + 1.0),
        0.5 * square,
    ]
    return (values, slopes)


def pair_force(centre, beside_all):
    separation = centre[:, :, :, None] - beside_all[:, :, None, :]
    distance_sq = jnp.sum(separation * separation, axis=0)
    weight = pair_strength * jnp.exp(-distance_sq / pair_range)
    return jnp.sum(weight[None] * separation, axis=3)


def domain_force(local_positions, neighbours):
    tile_count = neighbours.shape[0]
    bead_total = local_positions.shape[1]
    shaped = local_positions.reshape(3, bead_total, tile_count, TILE)

    def one_tile(tile_index):
        centre = lax.dynamic_index_in_dim(shaped, tile_index, 2, keepdims=False)
        beside_all = jnp.take(shaped, neighbours[tile_index], axis=2).reshape(
            3, bead_total, NBR * TILE
        )
        return pair_force(centre, beside_all)

    forces = lax.map(one_tile, jnp.arange(tile_count, dtype=jnp.int32))
    return jnp.moveaxis(forces, 0, 2).reshape(3, bead_total, tile_count * TILE)


def grid_positions(target, cells, offsets, planes):
    first = (target * planes + cells[0]).astype(jnp.float32) + offsets[0]
    second = cells[1].astype(jnp.float32) + offsets[1]
    third = cells[2].astype(jnp.float32) + offsets[2]
    return jnp.stack([first, second, third])


def real_waves(length):
    half = length // 2
    row = np.arange(length)
    wave = np.where(row <= half, row, row - half)
    angle = (wave[:, None] * np.arange(length)[None, :] % length) * (2.0 * math.pi / length)
    table = np.where((row <= half)[:, None], np.cos(angle), np.sin(angle))
    count = np.where((wave == 0) | (wave == half), 1.0, 2.0)
    return table, wave, count


def split_table(table):
    high = table.astype(jnp.bfloat16)
    low = (table - high.astype(np.float64)).astype(jnp.bfloat16)
    return high, low


def split(value):
    high = value.astype(jnp.bfloat16)
    low = (value - high.astype(jnp.float32)).astype(jnp.bfloat16)
    return high, low


def dot3(left, right, dims):
    def one(a, b):
        return lax.dot_general(a, b, (dims, ((), ())), preferred_element_type=jnp.float32)

    return one(left[0], right[0]) + (one(left[0], right[1]) + one(left[1], right[0]))


def stencil(position, length, with_slope):
    lowest = jnp.floor(position)
    values, slopes = spline(position - lowest)
    cell = lax.broadcasted_iota(jnp.int32, (length, position.shape[1]), 0)
    step = (cell - (lowest.astype(jnp.int32) - 1)) & (length - 1)
    hits = [step == offset for offset in range(4)]

    def dense(members):
        out = jnp.zeros(step.shape, jnp.float32)
        for offset in range(4):
            out = jnp.where(hits[offset], members[offset], out)
        return out

    return (dense(values), dense(slopes)) if with_slope else (dense(values),)


def mesh_kernel(chunks, group, fields, rxh, rxl, ryh, ryl, rzh, rzl, screen, out, total, gh, gl, xs, xd):
    step = pl.program_id(0)
    nx = rxh.shape[0]
    ny = ryh.shape[0]
    atoms = fields.shape[1]
    rows = group * ny
    nn = ((1,), (0,))
    nt = ((1,), (1,))

    def along(high, low, dense):
        return dot3((high[...], low[...]), split(dense), nn)

    @pl.when(step == 0)
    def _():
        total[...] = jnp.zeros_like(total)

    @pl.when(step < chunks)
    def _():
        xs[...] = along(rxh, rxl, stencil(fields[1:2, :], GX, False)[0]) * fields[0:1, :]
        ys = along(ryh, ryl, stencil(fields[2:3, :], GY, False)[0])
        zs = split(along(rzh, rzl, stencil(fields[3:4, :], GZ, False)[0]))

        def body(index, carry):
            parts = [xs[pl.ds(index * group + j, 1), :] * ys for j in range(group)]
            pair = split(jnp.concatenate(parts, axis=0))
            where = pl.ds(pl.multiple_of(index * rows, rows), rows)
            total[where, :] += dot3(pair, zs, nt)
            return carry

        lax.fori_loop(0, nx // group, body, 0)

    @pl.when(step == chunks - 1)
    def _():
        def body(index, carry):
            where = pl.ds(pl.multiple_of(index * rows, rows), rows)
            high, low = split(total[where, :] * screen[where, :])
            gh[where, :] = high
            gl[where, :] = low
            return carry

        lax.fori_loop(0, nx // group, body, 0)

    @pl.when(step >= chunks)
    def _():
        value, slope = stencil(fields[1:2, :], GX, True)
        xs[...] = along(rxh, rxl, value)
        xd[...] = along(rxh, rxl, slope)
        value, slope = stencil(fields[2:3, :], GY, True)
        ys = along(ryh, ryl, value)
        yd = along(ryh, ryl, slope)
        value, slope = stencil(fields[3:4, :], GZ, True)
        zs = split(along(rzh, rzl, value))
        zd = split(along(rzh, rzl, slope))

        def body(index, carry):
            force_x, force_y, force_z = carry
            where = pl.ds(pl.multiple_of(index * rows, rows), rows)
            filtered = (gh[where, :], gl[where, :])
            plain = dot3(filtered, zs, nn)
            steep = dot3(filtered, zd, nn)
            for j in range(group):
                own = plain[j * ny : (j + 1) * ny]
                x_here = xs[pl.ds(index * group + j, 1), :]
                force_x += xd[pl.ds(index * group + j, 1), :] * jnp.sum(own * ys, axis=0, keepdims=True)
                force_y += x_here * jnp.sum(own * yd, axis=0, keepdims=True)
                force_z += x_here * jnp.sum(
                    steep[j * ny : (j + 1) * ny] * ys, axis=0, keepdims=True
                )
            return force_x, force_y, force_z

        empty = jnp.zeros((1, atoms), jnp.float32)
        found = lax.fori_loop(0, nx // group, body, (empty, empty, empty))
        for c in range(3):
            out[c : c + 1, :] = -fields[0:1, :] * found[c]


def mesh_forces(fields, row_x, row_y, nx, ny):
    table_x, wave_x, count_x = real_waves(GX)
    table_y, wave_y, count_y = real_waves(GY)
    table_z, wave_z, count_z = real_waves(GZ)

    def rows_of(values, first, count):
        return lax.dynamic_slice_in_dim(jnp.asarray(values), first, count, 0)

    own = [rows_of(part, row_x, nx) for part in split_table(table_x)]
    own += [rows_of(part, row_y, ny) for part in split_table(table_y)]
    own += [jnp.asarray(part) for part in split_table(table_z)]
    square_x = rows_of((wave_x**2).astype(np.float32), row_x, nx)
    square_y = rows_of((wave_y**2).astype(np.float32), row_y, ny)
    times_x = rows_of((count_x / float(GX)).astype(np.float32), row_x, nx)
    times_y = rows_of((count_y / float(GY)).astype(np.float32), row_y, ny)
    square_z = jnp.asarray((wave_z**2).astype(np.float32))
    times_z = jnp.asarray((count_z / float(GZ)).astype(np.float32))
    square = (square_x[:, None] + square_y[None, :]).reshape(nx * ny, 1) + square_z[None, :]
    times = (times_x[:, None] * times_y[None, :]).reshape(nx * ny, 1) * times_z[None, :]
    centre = square == 0.0
    screen = jnp.where(
        centre,
        0.0,
        coulomb_scale
        * jnp.exp(-square / (2.0 * screen_width * screen_width))
        / jnp.where(centre, 1.0, square),
    )
    screen = screen * times

    atoms = fields.shape[1]
    width = min(512, atoms)
    chunks = atoms // width
    group = min(8, nx)
    full = lambda array: pl.BlockSpec(array.shape, lambda s: (0, 0))
    operands = [fields, *own, screen]
    return pl.pallas_call(
        functools.partial(mesh_kernel, chunks, group),
        grid=(2 * chunks,),
        out_shape=jax.ShapeDtypeStruct((3, atoms), jnp.float32),
        in_specs=[pl.BlockSpec((4, width), lambda s: (0, s % chunks))]
        + [full(array) for array in operands[1:]],
        out_specs=pl.BlockSpec((3, width), lambda s: (0, jnp.maximum(s - chunks, 0))),
        scratch_shapes=[
            pltpu.VMEM((nx * ny, GZ), jnp.float32),
            pltpu.VMEM((nx * ny, GZ), jnp.bfloat16),
            pltpu.VMEM((nx * ny, GZ), jnp.bfloat16),
            pltpu.VMEM((nx, width), jnp.float32),
            pltpu.VMEM((nx, width), jnp.float32),
        ],
        compiler_params=pltpu.CompilerParams(
            dimension_semantics=("arbitrary",), vmem_limit_bytes=48 * 1024 * 1024
        ),
        cost_estimate=pl.CostEstimate(
            flops=18 * nx * ny * GZ * atoms, bytes_accessed=8 * nx * ny * GZ, transcendentals=0
        ),
    )(*operands)


def step_tables(bead_total):
    mode = np.arange(bead_total)
    angle = (mode[:, None] * mode[None, :] % bead_total) * (2.0 * math.pi / bead_total)
    middle = bead_total // 2
    scaled = math.sqrt(2.0 / bead_total)
    column = mode[:, None]
    matrix = np.where(
        column == 0,
        1.0 / math.sqrt(bead_total),
        np.where(
            column < middle,
            scaled * np.cos(angle),
            np.where(
                column == middle, np.cos(angle) / math.sqrt(bead_total), scaled * np.sin(angle)
            ),
        ),
    )
    half = 0.5 * time_step
    frequency = 2.0 * polymer_frequency * np.sin(mode * (math.pi / bead_total))
    cosine = np.cos(frequency * half)
    drift = np.where(mode == 0, half, np.sin(frequency * half) / np.where(mode == 0, 1.0, frequency))
    pull = frequency * np.sin(frequency * half)
    friction = np.where(mode == 0, centroid_friction, 2.0 * frequency)
    damping = np.exp(-friction * time_step)
    kick = np.sqrt(1.0 - damping * damping)
    factors = [
        [cosine * cosine - drift * damping * pull, drift * cosine * (1.0 + damping), drift * kick],
        [-cosine * pull * (1.0 + damping), cosine * damping * cosine - pull * drift, cosine * kick],
    ]
    tables = np.stack(
        [
            np.stack(
                [
                    matrix.T @ (row[0][:, None] * matrix),
                    matrix.T @ (row[1][:, None] * matrix),
                    matrix.T * row[2][None, :],
                ]
            )
            for row in factors
        ]
    )
    return tables.astype(np.float32), (float(factors[0][1][0]), float(factors[1][1][0]))


def per_device(positions, momenta, noise, charges, slab_route, cells, offsets, nbr_tiles):
    grid_count = lax.axis_size("grid")
    bead_count = lax.axis_size("bead")
    grid_rank = lax.axis_index("grid")
    bead_rank = lax.axis_index("bead")
    beads_local = positions.shape[1]
    nx = GX // grid_count
    ny = GY // bead_count
    half_step = 0.5 * time_step

    grid_pos = grid_positions(slab_route[:, 0], cells, offsets, nx)
    fields = jnp.concatenate([charges[None, :], grid_pos], axis=0)
    fields = lax.all_gather(fields, "grid", axis=1, tiled=True)
    partial = mesh_forces(fields, grid_rank * nx, bead_rank * ny, nx, ny)
    mesh_force = lax.psum_scatter(partial, "grid", scatter_dimension=1, tiled=True)
    mesh_force = half_step * lax.psum(mesh_force, "bead")

    kicked = momenta + half_step * domain_force(positions, nbr_tiles)
    sources = lax.all_gather(
        jnp.stack([positions, kicked, noise]), "bead", axis=2, tiled=True
    )
    tables, (centre_q, centre_p) = step_tables(beads_local * bead_count)
    own = lax.dynamic_slice_in_dim(jnp.asarray(tables), bead_rank * beads_local, beads_local, 2)
    stepped = jnp.einsum("okbm,kcma->ocba", own, sources, precision=highest)
    return (
        stepped[0] + centre_q * mesh_force[:, None, :],
        stepped[1] + centre_p * mesh_force[:, None, :],
    )


def solution(mesh):
    in_specs = (
        P(None, "bead", "grid"),
        P(None, "bead", "grid"),
        P(None, "bead", "grid"),
        P("grid"),
        P("grid", None),
        P(None, "grid"),
        P(None, "grid"),
        P("grid", None),
    )
    out_specs = (P(None, "bead", "grid"), P(None, "bead", "grid"))
    return jax.shard_map(
        per_device, mesh=mesh, in_specs=in_specs, out_specs=out_specs, check_vma=False
    )
```

```python
import functools
import math

import jax
import jax.numpy as jnp
import numpy as np
from jax import lax
from jax.experimental import pallas as pl
from jax.experimental.pallas import tpu as pltpu
from jax.sharding import PartitionSpec as P

GX = 256
GY = 256
GZ = 256
BEADS = 32
TILE = 128
NBR = 4


highest = lax.Precision.HIGHEST
time_step = 0.5
polymer_frequency = 1.0
centroid_friction = 0.5
coulomb_scale = 100000.0
screen_width = 200.0
pair_strength = 1.0 / 128.0
pair_range = 4.0


def spline(fraction):
    remain = 1.0 - fraction
    square = fraction * fraction
    cubic = square * fraction
    values = [
        remain * remain * remain / 6.0,
        (3.0 * cubic - 6.0 * square + 4.0) / 6.0,
        (-3.0 * cubic + 3.0 * square + 3.0 * fraction + 1.0) / 6.0,
        cubic / 6.0,
    ]
    slopes = [
        -0.5 * remain * remain,
        0.5 * (3.0 * square - 4.0 * fraction),
        0.5 * (-3.0 * square + 2.0 * fraction + 1.0),
        0.5 * square,
    ]
    return (values, slopes)


def pair_kernel(counts, places, momenta, kicked):
    beads, atoms = places.shape[1:]
    tiles = atoms // TILE
    across = [places[c].T for c in range(3)]

    def body(t, carry):
        where = pl.ds(pl.multiple_of(t * TILE, TILE), TILE)
        for b in range(beads):
            centre = [places[c, b : b + 1, where] for c in range(3)]
            sums = [jnp.zeros((8, TILE), jnp.float32) for _ in range(3)]
            for m in range(tiles):
                apart = [
                    centre[c] - across[c][m * TILE : (m + 1) * TILE, b : b + 1] for c in range(3)
                ]
                square = apart[0] * apart[0] + apart[1] * apart[1] + apart[2] * apart[2]
                weight = jnp.exp(square * (-1.0 / pair_range))
                for c in range(3):
                    part = jnp.sum((weight * apart[c]).reshape(TILE // 8, 8, TILE), axis=0)
                    sums[c] = sums[c] + counts[t, m] * part
            for c in range(3):
                force = jnp.sum(sums[c], axis=0, keepdims=True)
                kicked[c, b : b + 1, where] = momenta[c, b : b + 1, where] + force
        return carry

    lax.fori_loop(0, tiles, body, 0)


def kick_short(positions, momenta, neighbours):
    tiles = neighbours.shape[0]
    listed = neighbours[:, :, None] == jnp.arange(tiles, dtype=jnp.int32)
    counts = jnp.sum(listed.astype(jnp.float32), axis=1) * (0.5 * time_step * pair_strength)
    pairs = positions.shape[1] * positions.shape[2] ** 2
    vmem = pl.BlockSpec(memory_space=pltpu.VMEM)
    return pl.pallas_call(
        pair_kernel,
        out_shape=jax.ShapeDtypeStruct(momenta.shape, jnp.float32),
        in_specs=[pl.BlockSpec(memory_space=pltpu.SMEM), vmem, vmem],
        out_specs=vmem,
        cost_estimate=pl.CostEstimate(
            flops=20 * pairs, bytes_accessed=12 * positions.size, transcendentals=pairs
        ),
    )(counts, positions, momenta)


def grid_positions(target, cells, offsets, planes):
    first = (target * planes + cells[0]).astype(jnp.float32) + offsets[0]
    second = cells[1].astype(jnp.float32) + offsets[1]
    third = cells[2].astype(jnp.float32) + offsets[2]
    return jnp.stack([first, second, third])


def real_waves(length):
    half = length // 2
    row = np.arange(length)
    wave = np.where(row <= half, row, row - half)
    angle = (wave[:, None] * np.arange(length)[None, :] % length) * (2.0 * math.pi / length)
    table = np.where((row <= half)[:, None], np.cos(angle), np.sin(angle))
    count = np.where((wave == 0) | (wave == half), 1.0, 2.0)
    return table, wave, count


def split_table(table):
    high = table.astype(jnp.bfloat16)
    low = (table - high.astype(np.float64)).astype(jnp.bfloat16)
    return high, low


def split(value):
    high = value.astype(jnp.bfloat16)
    low = (value - high.astype(jnp.float32)).astype(jnp.bfloat16)
    return high, low


def dot3(left, right, dims):
    def one(a, b):
        return lax.dot_general(a, b, (dims, ((), ())), preferred_element_type=jnp.float32)

    return one(left[0], right[0]) + (one(left[0], right[1]) + one(left[1], right[0]))


def stencil(position, length, with_slope):
    lowest = jnp.floor(position)
    values, slopes = spline(position - lowest)
    cell = lax.broadcasted_iota(jnp.int32, (length, position.shape[1]), 0)
    step = (cell - (lowest.astype(jnp.int32) - 1)) & (length - 1)
    hits = [step == offset for offset in range(4)]

    def dense(members):
        out = jnp.zeros(step.shape, jnp.float32)
        for offset in range(4):
            out = jnp.where(hits[offset], members[offset], out)
        return out

    return (dense(values), dense(slopes)) if with_slope else (dense(values),)


def mesh_kernel(chunks, group, fields, rxh, rxl, ryh, ryl, rzh, rzl, screen, out, total, gh, gl, xs, xd):
    step = pl.program_id(0)
    nx = rxh.shape[0]
    ny = ryh.shape[0]
    atoms = fields.shape[1]
    rows = group * ny
    nn = ((1,), (0,))
    nt = ((1,), (1,))

    def along(high, low, dense):
        return dot3((high[...], low[...]), split(dense), nn)

    @pl.when(step == 0)
    def _():
        total[...] = jnp.zeros_like(total)

    @pl.when(step < chunks)
    def _():
        xs[...] = along(rxh, rxl, stencil(fields[1:2, :], GX, False)[0]) * fields[0:1, :]
        ys = along(ryh, ryl, stencil(fields[2:3, :], GY, False)[0])
        zs = split(along(rzh, rzl, stencil(fields[3:4, :], GZ, False)[0]))

        def body(index, carry):
            parts = [xs[pl.ds(index * group + j, 1), :] * ys for j in range(group)]
            pair = split(jnp.concatenate(parts, axis=0))
            where = pl.ds(pl.multiple_of(index * rows, rows), rows)
            total[where, :] += dot3(pair, zs, nt)
            return carry

        lax.fori_loop(0, nx // group, body, 0)

    @pl.when(step == chunks - 1)
    def _():
        def body(index, carry):
            where = pl.ds(pl.multiple_of(index * rows, rows), rows)
            high, low = split(total[where, :] * screen[where, :])
            gh[where, :] = high
            gl[where, :] = low
            return carry

        lax.fori_loop(0, nx // group, body, 0)

    @pl.when(step >= chunks)
    def _():
        value, slope = stencil(fields[1:2, :], GX, True)
        xs[...] = along(rxh, rxl, value)
        xd[...] = along(rxh, rxl, slope)
        value, slope = stencil(fields[2:3, :], GY, True)
        ys = along(ryh, ryl, value)
        yd = along(ryh, ryl, slope)
        value, slope = stencil(fields[3:4, :], GZ, True)
        zs = split(along(rzh, rzl, value))
        zd = split(along(rzh, rzl, slope))

        def body(index, carry):
            force_x, force_y, force_z = carry
            where = pl.ds(pl.multiple_of(index * rows, rows), rows)
            filtered = (gh[where, :], gl[where, :])
            plain = dot3(filtered, zs, nn)
            steep = dot3(filtered, zd, nn)
            for j in range(group):
                own = plain[j * ny : (j + 1) * ny]
                x_here = xs[pl.ds(index * group + j, 1), :]
                force_x += xd[pl.ds(index * group + j, 1), :] * jnp.sum(own * ys, axis=0, keepdims=True)
                force_y += x_here * jnp.sum(own * yd, axis=0, keepdims=True)
                force_z += x_here * jnp.sum(
                    steep[j * ny : (j + 1) * ny] * ys, axis=0, keepdims=True
                )
            return force_x, force_y, force_z

        empty = jnp.zeros((1, atoms), jnp.float32)
        found = lax.fori_loop(0, nx // group, body, (empty, empty, empty))
        for c in range(3):
            out[c : c + 1, :] = -fields[0:1, :] * found[c]


def mesh_forces(fields, row_x, row_y, nx, ny):
    table_x, wave_x, count_x = real_waves(GX)
    table_y, wave_y, count_y = real_waves(GY)
    table_z, wave_z, count_z = real_waves(GZ)

    def rows_of(values, first, count):
        return lax.dynamic_slice_in_dim(jnp.asarray(values), first, count, 0)

    own = [rows_of(part, row_x, nx) for part in split_table(table_x)]
    own += [rows_of(part, row_y, ny) for part in split_table(table_y)]
    own += [jnp.asarray(part) for part in split_table(table_z)]
    square_x = rows_of((wave_x**2).astype(np.float32), row_x, nx)
    square_y = rows_of((wave_y**2).astype(np.float32), row_y, ny)
    times_x = rows_of((count_x / float(GX)).astype(np.float32), row_x, nx)
    times_y = rows_of((count_y / float(GY)).astype(np.float32), row_y, ny)
    square_z = jnp.asarray((wave_z**2).astype(np.float32))
    times_z = jnp.asarray((count_z / float(GZ)).astype(np.float32))
    square = (square_x[:, None] + square_y[None, :]).reshape(nx * ny, 1) + square_z[None, :]
    times = (times_x[:, None] * times_y[None, :]).reshape(nx * ny, 1) * times_z[None, :]
    centre = square == 0.0
    screen = jnp.where(
        centre,
        0.0,
        coulomb_scale
        * jnp.exp(-square / (2.0 * screen_width * screen_width))
        / jnp.where(centre, 1.0, square),
    )
    screen = screen * times

    atoms = fields.shape[1]
    width = min(512, atoms)
    chunks = atoms // width
    group = min(8, nx)
    full = lambda array: pl.BlockSpec(array.shape, lambda s: (0, 0))
    operands = [fields, *own, screen]
    return pl.pallas_call(
        functools.partial(mesh_kernel, chunks, group),
        grid=(2 * chunks,),
        out_shape=jax.ShapeDtypeStruct((3, atoms), jnp.float32),
        in_specs=[pl.BlockSpec((4, width), lambda s: (0, s % chunks))]
        + [full(array) for array in operands[1:]],
        out_specs=pl.BlockSpec((3, width), lambda s: (0, jnp.maximum(s - chunks, 0))),
        scratch_shapes=[
            pltpu.VMEM((nx * ny, GZ), jnp.float32),
            pltpu.VMEM((nx * ny, GZ), jnp.bfloat16),
            pltpu.VMEM((nx * ny, GZ), jnp.bfloat16),
            pltpu.VMEM((nx, width), jnp.float32),
            pltpu.VMEM((nx, width), jnp.float32),
        ],
        compiler_params=pltpu.CompilerParams(
            dimension_semantics=("arbitrary",), vmem_limit_bytes=48 * 1024 * 1024
        ),
        cost_estimate=pl.CostEstimate(
            flops=18 * nx * ny * GZ * atoms, bytes_accessed=8 * nx * ny * GZ, transcendentals=0
        ),
    )(*operands)


def step_tables(bead_total):
    mode = np.arange(bead_total)
    angle = (mode[:, None] * mode[None, :] % bead_total) * (2.0 * math.pi / bead_total)
    middle = bead_total // 2
    scaled = math.sqrt(2.0 / bead_total)
    column = mode[:, None]
    matrix = np.where(
        column == 0,
        1.0 / math.sqrt(bead_total),
        np.where(
            column < middle,
            scaled * np.cos(angle),
            np.where(
                column == middle, np.cos(angle) / math.sqrt(bead_total), scaled * np.sin(angle)
            ),
        ),
    )
    half = 0.5 * time_step
    frequency = 2.0 * polymer_frequency * np.sin(mode * (math.pi / bead_total))
    cosine = np.cos(frequency * half)
    drift = np.where(mode == 0, half, np.sin(frequency * half) / np.where(mode == 0, 1.0, frequency))
    pull = frequency * np.sin(frequency * half)
    friction = np.where(mode == 0, centroid_friction, 2.0 * frequency)
    damping = np.exp(-friction * time_step)
    kick = np.sqrt(1.0 - damping * damping)
    factors = [
        [cosine * cosine - drift * damping * pull, drift * cosine * (1.0 + damping), drift * kick],
        [-cosine * pull * (1.0 + damping), cosine * damping * cosine - pull * drift, cosine * kick],
    ]
    tables = np.stack(
        [
            np.stack(
                [
                    matrix.T @ (row[0][:, None] * matrix),
                    matrix.T @ (row[1][:, None] * matrix),
                    matrix.T * row[2][None, :],
                ]
            )
            for row in factors
        ]
    )
    return tables.astype(np.float32), (float(factors[0][1][0]), float(factors[1][1][0]))


def per_device(positions, momenta, noise, charges, slab_route, cells, offsets, nbr_tiles):
    grid_count = lax.axis_size("grid")
    bead_count = lax.axis_size("bead")
    grid_rank = lax.axis_index("grid")
    bead_rank = lax.axis_index("bead")
    beads_local = positions.shape[1]
    nx = GX // grid_count
    ny = GY // bead_count
    half_step = 0.5 * time_step

    grid_pos = grid_positions(slab_route[:, 0], cells, offsets, nx)
    fields = jnp.concatenate([charges[None, :], grid_pos], axis=0)
    copies = jnp.broadcast_to(fields[:, None, :], (4, grid_count, charges.shape[0]))
    fields = lax.all_to_all(copies, "grid", split_axis=1, concat_axis=1, tiled=True)
    fields = fields.reshape(4, grid_count * charges.shape[0])
    partial = mesh_forces(fields, grid_rank * nx, bead_rank * ny, nx, ny)
    shares = lax.all_to_all(
        partial.reshape(3, grid_count, charges.shape[0]), "grid", split_axis=1, concat_axis=1, tiled=True
    )
    mesh_force = half_step * lax.psum(jnp.sum(shares, axis=1), "bead")

    kicked = kick_short(positions, momenta, nbr_tiles)
    sources = lax.all_gather(
        jnp.stack([positions, kicked, noise]), "bead", axis=2, tiled=True
    )
    tables, (centre_q, centre_p) = step_tables(beads_local * bead_count)
    own = lax.dynamic_slice_in_dim(jnp.asarray(tables), bead_rank * beads_local, beads_local, 2)
    stepped = jnp.einsum("okbm,kcma->ocba", own, sources, precision=highest)
    return (
        stepped[0] + centre_q * mesh_force[:, None, :],
        stepped[1] + centre_p * mesh_force[:, None, :],
    )


def solution(mesh):
    in_specs = (
        P(None, "bead", "grid"),
        P(None, "bead", "grid"),
        P(None, "bead", "grid"),
        P("grid"),
        P("grid", None),
        P(None, "grid"),
        P(None, "grid"),
        P("grid", None),
    )
    out_specs = (P(None, "bead", "grid"), P(None, "bead", "grid"))
    return jax.shard_map(
        per_device, mesh=mesh, in_specs=in_specs, out_specs=out_specs, check_vma=False
    )
```

```python
import functools
import math

import jax
import jax.numpy as jnp
import numpy as np
from jax import lax
from jax.experimental import pallas as pl
from jax.experimental.pallas import tpu as pltpu
from jax.sharding import PartitionSpec as P

GX = 256
GY = 256
GZ = 256
BEADS = 32
TILE = 128
NBR = 4


highest = lax.Precision.HIGHEST
time_step = 0.5
polymer_frequency = 1.0
centroid_friction = 0.5
coulomb_scale = 100000.0
screen_width = 200.0
pair_strength = 1.0 / 128.0
pair_range = 4.0


def spline(fraction):
    remain = 1.0 - fraction
    square = fraction * fraction
    cubic = square * fraction
    values = [
        remain * remain * remain / 6.0,
        (3.0 * cubic - 6.0 * square + 4.0) / 6.0,
        (-3.0 * cubic + 3.0 * square + 3.0 * fraction + 1.0) / 6.0,
        cubic / 6.0,
    ]
    slopes = [
        -0.5 * remain * remain,
        0.5 * (3.0 * square - 4.0 * fraction),
        0.5 * (-3.0 * square + 2.0 * fraction + 1.0),
        0.5 * square,
    ]
    return (values, slopes)


def pair_kernel(counts, places, momenta, kicked):
    beads, atoms = places.shape[1:]
    tiles = atoms // TILE
    across = [places[c].T for c in range(3)]

    def body(t, carry):
        where = pl.ds(pl.multiple_of(t * TILE, TILE), TILE)
        for b in range(beads):
            centre = [places[c, b : b + 1, where] for c in range(3)]
            sums = [jnp.zeros((8, TILE), jnp.float32) for _ in range(3)]
            for m in range(tiles):
                apart = [
                    centre[c] - across[c][m * TILE : (m + 1) * TILE, b : b + 1] for c in range(3)
                ]
                square = apart[0] * apart[0] + apart[1] * apart[1] + apart[2] * apart[2]
                weight = jnp.exp(square * (-1.0 / pair_range))
                for c in range(3):
                    part = jnp.sum((weight * apart[c]).reshape(TILE // 8, 8, TILE), axis=0)
                    sums[c] = sums[c] + counts[t, m] * part
            for c in range(3):
                force = jnp.sum(sums[c], axis=0, keepdims=True)
                kicked[c, b : b + 1, where] = momenta[c, b : b + 1, where] + force
        return carry

    lax.fori_loop(0, tiles, body, 0)


def kick_short(positions, momenta, neighbours):
    tiles = neighbours.shape[0]
    listed = neighbours[:, :, None] == jnp.arange(tiles, dtype=jnp.int32)
    counts = jnp.sum(listed.astype(jnp.float32), axis=1) * (0.5 * time_step * pair_strength)
    pairs = positions.shape[1] * positions.shape[2] ** 2
    vmem = pl.BlockSpec(memory_space=pltpu.VMEM)
    return pl.pallas_call(
        pair_kernel,
        out_shape=jax.ShapeDtypeStruct(momenta.shape, jnp.float32),
        in_specs=[pl.BlockSpec(memory_space=pltpu.SMEM), vmem, vmem],
        out_specs=vmem,
        cost_estimate=pl.CostEstimate(
            flops=20 * pairs, bytes_accessed=12 * positions.size, transcendentals=pairs
        ),
    )(counts, positions, momenta)


def grid_positions(target, cells, offsets, planes):
    first = (target * planes + cells[0]).astype(jnp.float32) + offsets[0]
    second = cells[1].astype(jnp.float32) + offsets[1]
    third = cells[2].astype(jnp.float32) + offsets[2]
    return jnp.stack([first, second, third])


def real_waves(length):
    half = length // 2
    row = np.arange(length)
    wave = np.where(row <= half, row, row - half)
    angle = (wave[:, None] * np.arange(length)[None, :] % length) * (2.0 * math.pi / length)
    table = np.where((row <= half)[:, None], np.cos(angle), np.sin(angle))
    count = np.where((wave == 0) | (wave == half), 1.0, 2.0)
    return table, wave, count


def split_table(table):
    high = table.astype(jnp.bfloat16)
    low = (table - high.astype(np.float64)).astype(jnp.bfloat16)
    return high, low


def split(value):
    high = value.astype(jnp.bfloat16)
    low = (value - high.astype(jnp.float32)).astype(jnp.bfloat16)
    return high, low


def dot3(left, right, dims):
    def one(a, b):
        return lax.dot_general(a, b, (dims, ((), ())), preferred_element_type=jnp.float32)

    return one(left[0], right[0]) + (one(left[0], right[1]) + one(left[1], right[0]))


def stencil(position, length, with_slope):
    lowest = jnp.floor(position)
    values, slopes = spline(position - lowest)
    cell = lax.broadcasted_iota(jnp.int32, (length, position.shape[1]), 0)
    step = (cell - (lowest.astype(jnp.int32) - 1)) & (length - 1)
    step = step.astype(jnp.int16)
    hits = [step == jnp.asarray(offset, step.dtype) for offset in range(4)]

    def dense(members):
        out = jnp.zeros(step.shape, jnp.bfloat16)
        for offset in range(4):
            out = jnp.where(hits[offset], members[offset], out)
        return out

    def both(members):
        halves = [split(member) for member in members]
        return dense([half[0] for half in halves]), dense([half[1] for half in halves])

    return (both(values), both(slopes)) if with_slope else (both(values),)


def mesh_kernel(chunks, group, fields, rxh, rxl, ryh, ryl, rzh, rzl, screen, out, total, gh, gl, xs, xd):
    step = pl.program_id(0)
    nx = rxh.shape[0]
    ny = ryh.shape[0]
    atoms = fields.shape[1]
    rows = group * ny
    nn = ((1,), (0,))
    nt = ((1,), (1,))

    def along(high, low, dense):
        return dot3((high[...], low[...]), dense, nn)

    @pl.when(step == 0)
    def _():
        total[...] = jnp.zeros_like(total)

    @pl.when(step < chunks)
    def _():
        xs[...] = along(rxh, rxl, stencil(fields[1:2, :], GX, False)[0]) * fields[0:1, :]
        ys = along(ryh, ryl, stencil(fields[2:3, :], GY, False)[0])
        zs = split(along(rzh, rzl, stencil(fields[3:4, :], GZ, False)[0]))

        def body(index, carry):
            parts = [xs[pl.ds(index * group + j, 1), :] * ys for j in range(group)]
            pair = split(jnp.concatenate(parts, axis=0))
            where = pl.ds(pl.multiple_of(index * rows, rows), rows)
            total[where, :] += dot3(pair, zs, nt)
            return carry

        lax.fori_loop(0, nx // group, body, 0, unroll=True)

    @pl.when(step == chunks - 1)
    def _():
        def body(index, carry):
            where = pl.ds(pl.multiple_of(index * rows, rows), rows)
            high, low = split(total[where, :] * screen[where, :])
            gh[where, :] = high
            gl[where, :] = low
            return carry

        lax.fori_loop(0, nx // group, body, 0)

    @pl.when(step >= chunks)
    def _():
        value, slope = stencil(fields[1:2, :], GX, True)
        xs[...] = along(rxh, rxl, value)
        xd[...] = along(rxh, rxl, slope)
        value, slope = stencil(fields[2:3, :], GY, True)
        ys = along(ryh, ryl, value)
        yd = along(ryh, ryl, slope)
        value, slope = stencil(fields[3:4, :], GZ, True)
        zs = split(along(rzh, rzl, value))
        zd = split(along(rzh, rzl, slope))

        def body(index, carry):
            force_x, force_y, force_z = carry
            where = pl.ds(pl.multiple_of(index * rows, rows), rows)
            filtered = (gh[where, :], gl[where, :])
            plain = dot3(filtered, zs, nn)
            steep = dot3(filtered, zd, nn)
            for j in range(group):
                own = plain[j * ny : (j + 1) * ny]
                x_here = xs[pl.ds(index * group + j, 1), :]
                force_x += xd[pl.ds(index * group + j, 1), :] * jnp.sum(own * ys, axis=0, keepdims=True)
                force_y += x_here * jnp.sum(own * yd, axis=0, keepdims=True)
                force_z += x_here * jnp.sum(
                    steep[j * ny : (j + 1) * ny] * ys, axis=0, keepdims=True
                )
            return force_x, force_y, force_z

        empty = jnp.zeros((1, atoms), jnp.float32)
        found = lax.fori_loop(0, nx // group, body, (empty, empty, empty), unroll=True)
        for c in range(3):
            out[c : c + 1, :] = -fields[0:1, :] * found[c]


def mesh_forces(fields, row_x, row_y, nx, ny):
    table_x, wave_x, count_x = real_waves(GX)
    table_y, wave_y, count_y = real_waves(GY)
    table_z, wave_z, count_z = real_waves(GZ)

    def rows_of(values, first, count):
        return lax.dynamic_slice_in_dim(jnp.asarray(values), first, count, 0)

    own = [rows_of(part, row_x, nx) for part in split_table(table_x)]
    own += [rows_of(part, row_y, ny) for part in split_table(table_y)]
    own += [jnp.asarray(part) for part in split_table(table_z)]
    square_x = rows_of((wave_x**2).astype(np.float32), row_x, nx)
    square_y = rows_of((wave_y**2).astype(np.float32), row_y, ny)
    times_x = rows_of((count_x / float(GX)).astype(np.float32), row_x, nx)
    times_y = rows_of((count_y / float(GY)).astype(np.float32), row_y, ny)
    square_z = jnp.asarray((wave_z**2).astype(np.float32))
    times_z = jnp.asarray((count_z / float(GZ)).astype(np.float32))
    square = (square_x[:, None] + square_y[None, :]).reshape(nx * ny, 1) + square_z[None, :]
    times = (times_x[:, None] * times_y[None, :]).reshape(nx * ny, 1) * times_z[None, :]
    centre = square == 0.0
    screen = jnp.where(
        centre,
        0.0,
        coulomb_scale
        * jnp.exp(-square / (2.0 * screen_width * screen_width))
        / jnp.where(centre, 1.0, square),
    )
    screen = screen * times

    atoms = fields.shape[1]
    width = min(512, atoms)
    chunks = atoms // width
    group = min(8, nx)
    full = lambda array: pl.BlockSpec(array.shape, lambda s: (0, 0))
    operands = [fields, *own, screen]
    return pl.pallas_call(
        functools.partial(mesh_kernel, chunks, group),
        grid=(2 * chunks,),
        out_shape=jax.ShapeDtypeStruct((3, atoms), jnp.float32),
        in_specs=[pl.BlockSpec((4, width), lambda s: (0, s % chunks))]
        + [full(array) for array in operands[1:]],
        out_specs=pl.BlockSpec((3, width), lambda s: (0, jnp.maximum(s - chunks, 0))),
        scratch_shapes=[
            pltpu.VMEM((nx * ny, GZ), jnp.float32),
            pltpu.VMEM((nx * ny, GZ), jnp.bfloat16),
            pltpu.VMEM((nx * ny, GZ), jnp.bfloat16),
            pltpu.VMEM((nx, width), jnp.float32),
            pltpu.VMEM((nx, width), jnp.float32),
        ],
        compiler_params=pltpu.CompilerParams(
            dimension_semantics=("arbitrary",), vmem_limit_bytes=48 * 1024 * 1024
        ),
        cost_estimate=pl.CostEstimate(
            flops=18 * nx * ny * GZ * atoms, bytes_accessed=8 * nx * ny * GZ, transcendentals=0
        ),
    )(*operands)


def step_tables(bead_total):
    mode = np.arange(bead_total)
    angle = (mode[:, None] * mode[None, :] % bead_total) * (2.0 * math.pi / bead_total)
    middle = bead_total // 2
    scaled = math.sqrt(2.0 / bead_total)
    column = mode[:, None]
    matrix = np.where(
        column == 0,
        1.0 / math.sqrt(bead_total),
        np.where(
            column < middle,
            scaled * np.cos(angle),
            np.where(
                column == middle, np.cos(angle) / math.sqrt(bead_total), scaled * np.sin(angle)
            ),
        ),
    )
    half = 0.5 * time_step
    frequency = 2.0 * polymer_frequency * np.sin(mode * (math.pi / bead_total))
    cosine = np.cos(frequency * half)
    drift = np.where(mode == 0, half, np.sin(frequency * half) / np.where(mode == 0, 1.0, frequency))
    pull = frequency * np.sin(frequency * half)
    friction = np.where(mode == 0, centroid_friction, 2.0 * frequency)
    damping = np.exp(-friction * time_step)
    kick = np.sqrt(1.0 - damping * damping)
    factors = [
        [cosine * cosine - drift * damping * pull, drift * cosine * (1.0 + damping), drift * kick],
        [-cosine * pull * (1.0 + damping), cosine * damping * cosine - pull * drift, cosine * kick],
    ]
    tables = np.stack(
        [
            np.stack(
                [
                    matrix.T @ (row[0][:, None] * matrix),
                    matrix.T @ (row[1][:, None] * matrix),
                    matrix.T * row[2][None, :],
                ]
            )
            for row in factors
        ]
    )
    return tables.astype(np.float32), (float(factors[0][1][0]), float(factors[1][1][0]))


def per_device(positions, momenta, noise, charges, slab_route, cells, offsets, nbr_tiles):
    grid_count = lax.axis_size("grid")
    bead_count = lax.axis_size("bead")
    grid_rank = lax.axis_index("grid")
    bead_rank = lax.axis_index("bead")
    beads_local = positions.shape[1]
    nx = GX // grid_count
    ny = GY // bead_count
    half_step = 0.5 * time_step

    grid_pos = grid_positions(slab_route[:, 0], cells, offsets, nx)
    fields = jnp.concatenate([charges[None, :], grid_pos], axis=0)
    copies = jnp.broadcast_to(fields[:, None, :], (4, grid_count, charges.shape[0]))
    fields = lax.all_to_all(copies, "grid", split_axis=1, concat_axis=1, tiled=True)
    fields = fields.reshape(4, grid_count * charges.shape[0])
    partial = mesh_forces(fields, grid_rank * nx, bead_rank * ny, nx, ny)
    shares = lax.all_to_all(
        partial.reshape(3, grid_count, charges.shape[0]), "grid", split_axis=1, concat_axis=1, tiled=True
    )
    mesh_force = half_step * lax.psum(jnp.sum(shares, axis=1), "bead")

    kicked = kick_short(positions, momenta, nbr_tiles)
    sources = lax.all_gather(
        jnp.stack([positions, kicked, noise]), "bead", axis=2, tiled=True
    )
    tables, (centre_q, centre_p) = step_tables(beads_local * bead_count)
    own = lax.dynamic_slice_in_dim(jnp.asarray(tables), bead_rank * beads_local, beads_local, 2)
    stepped = jnp.einsum("okbm,kcma->ocba", own, sources, precision=highest)
    return (
        stepped[0] + centre_q * mesh_force[:, None, :],
        stepped[1] + centre_p * mesh_force[:, None, :],
    )


def solution(mesh):
    in_specs = (
        P(None, "bead", "grid"),
        P(None, "bead", "grid"),
        P(None, "bead", "grid"),
        P("grid"),
        P("grid", None),
        P(None, "grid"),
        P(None, "grid"),
        P("grid", None),
    )
    out_specs = (P(None, "bead", "grid"), P(None, "bead", "grid"))
    return jax.shard_map(
        per_device, mesh=mesh, in_specs=in_specs, out_specs=out_specs, check_vma=False
    )
```
